512 devices in a mesh: pair: 2 (over y_hi), blk: 32 (over y_lo, z), group: 8 (over x, core).
Axes of the slice: x: 4, y: 8 (y_hi: 2, y_lo: 4; y = y_hi * 4 + y_lo), z: 8, core: 2. Of those that a mesh axis runs over, the one named last changes fastest.
Arguments:
- codes: int32 [512, 1536, 256], P(('pair', 'blk', 'group')), may hold values from 0 to 255
- scales: int32 [512, 1536, 8], P(('pair', 'blk', 'group')), may hold values from -7 to 0
- inputs: bfloat16 [65536, 1536], P(('pair', 'blk', 'group')), may hold values from -6 to 6
- cotangent: bfloat16 [65536, 256], P(('pair', 'blk', 'group')), may hold values from -6 to 6
Outputs:
- earlier_grad: float32 [1536, 256], replicated
- current_grad: float32 [1536, 256], replicated
The draws below stay inside these ranges and needn't reach their ends.
All inputs are finite; a program needn't handle non-finite values.
Results may differ from the reference program's by a relative error of at most 0.0003.
Values sent between devices are 32-bit elements; how exact they have to be, the bound alone decides.
A program may use at most 64 MiB of HBM per device.

```python
import jax
import jax.numpy as jnp
from jax import lax

D = 1536
KVW = 256
BLOCK = 32
SOURCES = 512
TOKENS = 65536
N_PAIR = 2
N_BLK = 32
N_GROUP = 8


def place_ends(array, stream_key, least, top_value):
    index_at = [jax.random.randint(jax.random.fold_in(stream_key, axis), (), 0, length) for axis, length in enumerate(array.shape)]
    main_axis = array.shape.index(max(array.shape))
    neighbour = index_at[:main_axis] + [(index_at[main_axis] + 1) % array.shape[main_axis]] + index_at[main_axis + 1:]
    return array.at[tuple(index_at)].set(least).at[tuple(neighbour)].set(top_value)


def level_of(rng, extent, pieces, low, high):
    def one(position, blocks):
        draws = jax.random.uniform(jax.random.fold_in(jax.random.fold_in(rng, 6), position), (blocks,), jnp.float32, low / len(pieces), high / len(pieces))
        return jnp.repeat(jnp.exp(draws), extent[position] // blocks).reshape((-1,) + (1,) * (len(extent) - position - 1))

    factor_of = one(*pieces[0])
    for cut in pieces[1:]:
        factor_of = factor_of * one(*cut)
    return factor_of


def gaussian(stream_key, shape, scale, most, pieces=(), dtype=jnp.bfloat16):
    gain = level_of(stream_key, shape, pieces, -0.22, 0.18) if pieces else 1.0
    entries = jax.random.normal(stream_key, shape, jnp.float32) * scale * gain
    return jnp.minimum(jnp.maximum(entries, -most), most).astype(dtype)


def setup_inputs(seed: int = 0) -> dict:
    arg_keys = jax.random.split(jax.random.key(seed), 5)
    codes = place_ends(jax.random.randint(arg_keys[0], (SOURCES, D, KVW), 0, 256), jax.random.fold_in(arg_keys[0], 1), 0, 255).astype(jnp.int32)
    scales = place_ends(jax.random.randint(arg_keys[1], (SOURCES, D, KVW // BLOCK), -7, 1), jax.random.fold_in(arg_keys[1], 1), -7, 0).astype(jnp.int32)
    inputs = gaussian(arg_keys[2], (TOKENS, D), 1.0, 6.0, ((0, 512),))
    cotangent = gaussian(arg_keys[3], (TOKENS, KVW), 1.0, 6.0, ((0, 512),))
    return {"codes": codes, "scales": scales, "inputs": inputs, "cotangent": cotangent}


def decode(codes, scales):
    sign = 1.0 - 2.0 * (codes // 128).astype(jnp.float32)
    field = (codes // 8) % 16
    mant = (codes % 8).astype(jnp.float32)
    frac = jnp.where(field > 0, 8.0 + mant, mant)
    power = jnp.where(field > 0, field, 1) - 10
    expo = power + jnp.repeat(scales, BLOCK, axis=-1)
    return sign * frac * jnp.exp2(expo.astype(jnp.float32))


def reference(codes, scales, inputs, cotangent):
    def accumulate(total, member):
        return total + decode(member[0], member[1]), None

    total, unused = lax.scan(accumulate, jnp.zeros((D, KVW), jnp.float32), (codes, scales))
    count = N_PAIR * N_BLK * N_GROUP
    earlier_grad = total / count
    product = jnp.dot(inputs.T, cotangent, preferred_element_type=jnp.float32)
    current_grad = product / count
    return earlier_grad, current_grad
```

```python
import functools

import jax
import jax.numpy as jnp
from jax import lax
from jax.experimental import pallas as pl
from jax.experimental.pallas import tpu as pltpu
from jax.sharding import PartitionSpec as P

EVERY = ("pair", "blk", "group")
MESH_ID = pl.DeviceIdType.MESH
NX, NY, NZ = 4, 8, 8
RING = 8
HALF = RING // 2
BLOCK = 3
PAIR = 2 * BLOCK
CHUNK = RING * BLOCK
OWN = RING * CHUNK
ALL = 2 * OWN
SUBS = 4
OFFSETS = (2, 1, 3, 0)
TILE = (8, 128)


def steps_of(direction, sub):
    return HALF if (sub < SUBS // 2) == (direction == 0) else HALF - 1


def rem(a, n):
    return lax.rem(a, jnp.int32(n))


def div(a, n):
    return lax.div(a, jnp.int32(n))


def kernel(
    codes_ref, scales_ref, inputs_ref, cot_ref, out0, out1,
    codes_v, scales_v, inputs_v, cot_v,
    part0, part1, peer0, peer1, ring_in, ring_out, chunk_sum, block_in, x_in,
    load_sem, peer_sem, ring_sem, block_sem, x_sem, owner_sem, spread_sem, final_sem, send_sem,
):
    outs, parts, peers = (out0, out1), (part0, part1), (peer0, peer1)
    group = lax.axis_index("group")
    blk = lax.axis_index("blk")
    x, core = div(group, 2), rem(group, 2)
    y, z = lax.axis_index("pair") * 4 + div(blk, 8), rem(blk, 8)

    def device(x, y, z, core):
        return (div(y, 4), rem(y, 4) * 8 + z, x * 2 + core)

    def along_first(color, to):
        return device(x, to, z, core) if color == 0 else device(x, y, to, core)

    def along_second(color, to):
        return device(x, y, to, core) if color == 0 else device(x, to, z, core)

    first = (y, z)
    second = (z, y)
    partner = device(x, y, z, 1 - core)

    loads = [
        pltpu.make_async_copy(src, dst, load_sem.at[i])
        for i, (src, dst) in enumerate(
            ((codes_ref, codes_v), (scales_ref, scales_v), (inputs_ref, inputs_v), (cot_ref, cot_v))
        )
    ]
    for load in loads:
        load.start()

    barrier = pltpu.get_barrier_semaphore()
    greeted = [partner]
    greeted += [device(rem(x + d, NX), y, z, core) for d in range(1, NX)]
    greeted += [device(x, rem(y + d, NY), z, core) for d in range(1, NY)]
    greeted += [device(x, y, rem(z + d, NZ), core) for d in range(1, NZ)]
    for other in greeted:
        pl.semaphore_signal(barrier, inc=1, device_id=other, device_id_type=MESH_ID)

    for load in loads:
        load.wait()

    lane_block = lax.broadcasted_iota(jnp.int32, (8, 256), 1) // 32
    spread = (lane_block == lax.broadcasted_iota(jnp.int32, (8, 256), 0)).astype(jnp.float32)

    def compute(i, carry):
        rows = pl.ds(pl.multiple_of(i * 128, 128), 128)
        code = codes_v[rows, :]
        field = (code >> 3) & 15
        mant = code & 7
        magnitude = jnp.where(field > 0, mant + 8, mant) << jnp.maximum(field - 1, 0)
        signed = jnp.where(code >= 128, -magnitude, magnitude).astype(jnp.float32)
        powers = jnp.exp2((scales_v[:, rows] - 9).astype(jnp.float32))
        scale = lax.dot_general(
            powers, spread, (((0,), (0,)), ((), ())), preferred_element_type=jnp.float32
        )
        decoded = signed * scale
        product = lax.dot_general(
            inputs_v[:, rows], cot_v[...], (((0,), (0,)), ((), ())),
            preferred_element_type=jnp.float32,
        )
        for part, value in ((part0, decoded), (part1, product)):
            for r in range(16):
                for t in range(2):
                    part[32 * i + 2 * r + t] = value[8 * r : 8 * r + 8, 128 * t : 128 * t + 128]
        return carry

    lax.fori_loop(0, 12, compute, 0)

    pl.semaphore_wait(barrier, len(greeted))

    def send(src, dst, sent, received, to):
        pltpu.make_async_remote_copy(
            src_ref=src, dst_ref=dst, send_sem=sent, recv_sem=received,
            device_id=to, device_id_type=MESH_ID,
        ).start()

    def wait_for(ref, sem):
        pltpu.make_async_copy(ref, ref, sem).wait()

    reach = [HALF] + [s * d for d in range(HALF - 1, 0, -1) for s in (1, -1)] + [0]
    for d in reach:
        for color in range(2):
            at = rem(first[color] + d + RING, RING) * CHUNK
            send(
                parts[color].at[pl.ds((1 - core) * OWN + at, CHUNK)],
                peers[color].at[pl.ds(at, CHUNK)],
                send_sem.at[color, 0],
                peer_sem.at[color, d + HALF - 1],
                partner,
            )

    pairs = [[rem(div(second[q], 2) + o, SUBS) for o in OFFSETS] for q in range(2)]

    def chip_sum(color, chunk, sub):
        at = chunk * CHUNK + pairs[color][sub] * PAIR
        return parts[color][pl.ds(core * OWN + at, PAIR)] + peers[color][pl.ds(at, PAIR)]

    for step in range(HALF):
        left = HALF - step
        for d in ((HALF,) if left == HALF else (left, -left)):
            for color in range(2):
                wait_for(peers[color].at[pl.ds(0, CHUNK)], peer_sem.at[color, d + HALF - 1])
        for sub in range(SUBS):
            for color in range(2):
                for direction, sign in ((0, 1), (1, -1)):
                    if steps_of(direction, sub) < left:
                        continue
                    value = chip_sum(color, rem(first[color] + sign * left + RING, RING), sub)
                    if steps_of(direction, sub) > left:
                        arrived = ring_in.at[color, direction, step - 1, sub]
                        wait_for(arrived, ring_sem.at[color, direction, step - 1, sub])
                        value = value + arrived[...]
                    ring_out[color, direction, step, sub] = value
                    send(
                        ring_out.at[color, direction, step, sub],
                        ring_in.at[color, direction, step, sub],
                        send_sem.at[color, 1],
                        ring_sem.at[color, direction, step, sub],
                        along_first(color, rem(first[color] + sign + RING, RING)),
                    )

    for color in range(2):
        wait_for(peers[color].at[pl.ds(0, CHUNK)], peer_sem.at[color, HALF - 1])
    for sub in range(SUBS):
        for color in range(2):
            value = chip_sum(color, first[color], sub)
            for direction in range(2):
                arrived = ring_in.at[color, direction, HALF - 1, sub]
                wait_for(arrived, ring_sem.at[color, direction, HALF - 1, sub])
                value = value + arrived[...]
            chunk_sum[color, pl.ds(pairs[color][sub] * PAIR, PAIR)] = value
            if OFFSETS[sub]:
                owners = [pairs[color][sub] * 2, pairs[color][sub] * 2 + 1]
            else:
                owners = [second[color] + 1 - 2 * rem(second[color], 2)]
            for owner in owners:
                send(
                    chunk_sum.at[color, pl.ds(owner * BLOCK, BLOCK)],
                    block_in.at[color, rem(second[color] - owner + RING, RING) - 1],
                    send_sem.at[color, 2],
                    block_sem.at[color],
                    along_second(color, owner),
                )

    for color in range(2):
        wait_for(block_in.at[color], block_sem.at[color])
        value = chunk_sum[color, pl.ds(second[color] * BLOCK, BLOCK)]
        for slot in range(RING - 1):
            value = value + block_in[color, slot]
        x_in[color, x] = value
        for d in (2, 1, 3):
            send(
                x_in.at[color, x],
                x_in.at[color, x],
                send_sem.at[color, 3],
                x_sem.at[color],
                device(rem(x + d, NX), y, z, core),
            )

    def place(color, chunk):
        return core * OWN + chunk * CHUNK

    count = 2.0 * NX * NY * NZ
    for color in range(2):
        wait_for(x_in.at[color, pl.ds(0, NX - 1)], x_sem.at[color])
        total = x_in[color, 0]
        for k in range(1, NX):
            total = total + x_in[color, k]
        mine = pl.ds(place(color, first[color]) + second[color] * BLOCK, BLOCK)
        outs[color][mine] = total * (1.0 / count)
        for d in (4, 3, 5, 2, 6, 1, 7):
            other = rem(second[color] + d, RING)
            offset = rem(div(second[color], 2) - div(other, 2) + SUBS, SUBS)
            send(
                outs[color].at[mine],
                outs[color].at[mine],
                send_sem.at[color, 4],
                owner_sem.at[color, offset],
                along_second(color, other),
            )

    events = []
    for sub in range(SUBS):
        ready = {0: 1.9, 1: 3.1, 3: 3.1, 2: 4.0}[OFFSETS[sub]]
        for step in range(HALF + 1):
            events.append((ready + 1.9 * step, step, sub))
    for _, step, sub in sorted(events):
        for color in range(2):
            for direction, sign in ((0, 1), (1, -1)):
                if step > steps_of(direction, sub) or (step == 0 and direction == 1):
                    continue
                chunk = rem(first[color] - sign * step + RING, RING)
                here = outs[color].at[
                    pl.ds(place(color, chunk) + pairs[color][sub] * PAIR, PAIR)
                ]
                if step == 0:
                    size = PAIR if OFFSETS[sub] else BLOCK
                    wait_for(
                        outs[color].at[pl.ds(0, size)], owner_sem.at[color, OFFSETS[sub]]
                    )
                else:
                    wait_for(here, spread_sem.at[color, direction, step - 1, sub])
                for way, turn in ((0, 1), (1, -1)):
                    if (step == 0 or way == direction) and step < steps_of(way, sub):
                        send(
                            here,
                            here,
                            send_sem.at[color, 5],
                            spread_sem.at[color, way, step, sub],
                            along_first(color, rem(first[color] + turn + RING, RING)),
                        )
                send(here, here, send_sem.at[color, 6], final_sem.at[color], partner)

    sent = (OWN, 28 * PAIR, 7 * BLOCK, 3 * BLOCK, 7 * BLOCK, 28 * PAIR, OWN)
    for color in range(2):
        wait_for(outs[color].at[pl.ds(0, OWN)], final_sem.at[color])
        for kind, tiles in enumerate(sent):
            wait_for(parts[color].at[pl.ds(0, tiles)], send_sem.at[color, kind])


def summed(codes, scales, inputs, cotangent):
    tiles = jax.ShapeDtypeStruct((ALL, *TILE), jnp.float32)
    dma = pltpu.SemaphoreType.DMA
    return pl.pallas_call(
        kernel,
        name="sum_everywhere",
        out_shape=(tiles, tiles),
        in_specs=[pl.BlockSpec(memory_space=pltpu.HBM)] * 4,
        out_specs=[pl.BlockSpec(memory_space=pltpu.VMEM)] * 2,
        scratch_shapes=[
            pltpu.VMEM(codes.shape, jnp.int32),
            pltpu.VMEM(scales.shape, jnp.int32),
            pltpu.VMEM(inputs.shape, inputs.dtype),
            pltpu.VMEM(cotangent.shape, cotangent.dtype),
            pltpu.VMEM((ALL, *TILE), jnp.float32),
            pltpu.VMEM((ALL, *TILE), jnp.float32),
            pltpu.VMEM((OWN, *TILE), jnp.float32),
            pltpu.VMEM((OWN, *TILE), jnp.float32),
            pltpu.VMEM((2, 2, HALF, SUBS, PAIR, *TILE), jnp.float32),
            pltpu.VMEM((2, 2, HALF, SUBS, PAIR, *TILE), jnp.float32),
            pltpu.VMEM((2, CHUNK, *TILE), jnp.float32),
            pltpu.VMEM((2, RING - 1, BLOCK, *TILE), jnp.float32),
            pltpu.VMEM((2, NX, BLOCK, *TILE), jnp.float32),
            dma((4,)),
            dma((2, 2 * HALF)),
            dma((2, 2, HALF, SUBS)),
            dma((2,)),
            dma((2,)),
            dma((2, SUBS)),
            dma((2, 2, HALF, SUBS)),
            dma((2,)),
            dma((2, 7)),
        ],
        compiler_params=pltpu.CompilerParams(
            collective_id=0, has_side_effects=True, vmem_limit_bytes=40 << 20
        ),
    )(codes, scales, inputs, cotangent)


def untiled(tiles, shape):
    rows, columns = shape
    grid = tiles.reshape(rows // 8, columns // 128, *TILE)
    return grid.transpose(0, 2, 1, 3).reshape(shape)


def local(codes, scales, inputs, cotangent):
    shape = codes.shape[1:]
    earlier, current = summed(codes[0], scales[0].T, inputs, cotangent)
    return untiled(earlier, shape), untiled(current, shape)


def solution(mesh):
    in_specs = (
        P(EVERY, None, None),
        P(EVERY, None, None),
        P(EVERY, None),
        P(EVERY, None),
    )
    return jax.shard_map(
        local, mesh=mesh, in_specs=in_specs, out_specs=(P(), P()), check_vma=False
    )
```
